32 devices in a mesh: groups: 2 (over x), member: 2 (over core), tile: 8 (over z, y).
Axes of the slice: x: 2, y: 2, z: 4, core: 2. Of those that a mesh axis runs over, the one named last changes fastest.
Arguments:
- state: float32 [8, 4, 4, 512, 256], P(('groups', 'member'), None, None, 'tile'), parts along dimension 0, may hold values from -6 to 6
- perturbation: float32 [8, 4, 4, 512, 256], P(('groups', 'member'), None, None, 'tile'), parts along dimension 0, may hold values from -2 to 2
- ancestors: int32 [8], P('groups'), parts along dimension 0, may hold values from 0 to 3, as said below
Outputs:
- evolved: float32 [8, 4, 4, 512, 256], P(('groups', 'member'), None, None, 'tile'), parts along dimension 0
- observable: float32 [8], P(('groups', 'member')), parts along dimension 0
The draws below stay inside these ranges and needn't reach their ends.
There are 2 independent parts, one for each index of `groups`. The reference program is written for one: setup_inputs(seed, part) draws one part's arguments, and reference() takes and returns one part's arrays. A program takes and returns all parts, laid end to end along the dimension named above; each array names one. Nothing has to cross between parts.
Inputs may be any that keep to these rules, and one draw needn't show every extreme that they name: `ancestors`: surviving slots name themselves; every other slot names a surviving slot; at least two slots survive and at least one does not.
All inputs are finite; a program needn't handle non-finite values.
Results may differ from the reference program's by a relative error of at most 0.00002.
Values sent between devices are 32-bit elements; how exact they have to be, the bound alone decides.
A program may use at most 64 MiB of HBM per device.

```python
import jax
import jax.numpy as jnp

COLUMNS = 256
LEVELS = 4
FIELDS = 4
STEPS_EACH = 2
ENSEMBLE_SIZE = 4
ROWS = 512


def draw_ancestors(key, part):
    key_order = jax.random.fold_in(key, 11)
    count_key = jax.random.fold_in(key, 12)
    picking_key = jax.random.fold_in(key, 13)
    order = jax.random.permutation(key_order, ENSEMBLE_SIZE).astype(jnp.int32)
    member_ranks = jnp.argsort(order, stable=True).astype(jnp.int32)
    kept_members = jax.random.randint(count_key, (), 2, ENSEMBLE_SIZE, dtype=jnp.int32)
    living_members = member_ranks < kept_members
    chosen_members = jax.random.randint(picking_key, (ENSEMBLE_SIZE,), 0, kept_members, dtype=jnp.int32)
    sources = jnp.take(order, chosen_members)
    return jnp.where(living_members, jnp.arange(ENSEMBLE_SIZE, dtype=jnp.int32), sources).astype(jnp.int32)


def block_scale(rng, extent, cuts, least, high):
    gain, own = 1.0, jax.random.fold_in(rng, 6)
    for dim, shards_of in cuts:
        steps = jnp.exp(jax.random.uniform(jax.random.fold_in(own, dim), (shards_of,), jnp.float32, least / len(cuts), high / len(cuts)))
        gain = gain * jnp.repeat(steps, extent[dim] // shards_of).reshape([-1 if axis == dim else 1 for axis in range(len(extent))])
    return gain


def normal_values(key, extent, scale, reach, split=(), held_as=jnp.bfloat16):
    array = scale * jax.random.normal(key, extent, jnp.float32)
    if split:
        array = array * block_scale(key, extent, split, -0.22, 0.18)
    return jnp.clip(array, -reach, reach).astype(held_as)


def setup_inputs(seed: int = 0, part: int = 0) -> dict:
    arg_keys = jax.random.split(jax.random.key(seed), 4)
    part_keys = jax.random.split(jax.random.fold_in(arg_keys[3], part), 4)
    state = normal_values(part_keys[0], (ENSEMBLE_SIZE, FIELDS, LEVELS, ROWS, COLUMNS), 1.0, 6.0, ((0, 2), (3, 8)), jnp.float32)
    perturbation = normal_values(part_keys[1], (ENSEMBLE_SIZE, FIELDS, LEVELS, ROWS, COLUMNS), 0.3, 2.0, ((0, 2), (3, 8)), jnp.float32)
    ancestors = draw_ancestors(jax.random.fold_in(jax.random.fold_in(arg_keys[3], part), 71), part)
    return {"state": state, "perturbation": perturbation, "ancestors": ancestors}


TIME_STEP = 0.15
DIFFUSION = 0.2
MIXING = 0.1
CORIOLIS = 0.5
BUOYANCY_GAIN = 0.3
STRATIFICATION = 0.3
SATURATION = 0.5
LATENT = 0.5


def advance_core(padded):
    centre = padded[:, :, :, 2:-2, :]
    north_one = padded[:, :, :, 3:-1, :]
    south_one = padded[:, :, :, 1:-3, :]
    north_two = padded[:, :, :, 4:, :]
    south_two = padded[:, :, :, :-4, :]
    east_one = jnp.roll(centre, -1, axis=4)
    west_one = jnp.roll(centre, 1, axis=4)
    east_two = jnp.roll(centre, -2, axis=4)
    west_two = jnp.roll(centre, 2, axis=4)
    slope_y = (8.0 * (north_one - south_one) - (north_two - south_two)) / 12.0
    slope_x = (8.0 * (east_one - west_one) - (east_two - west_two)) / 12.0
    laplace = north_one + south_one + east_one + west_one - 4.0 * centre
    upper = jnp.concatenate([centre[:, :, 1:], centre[:, :, -1:]], axis=2)
    lower = jnp.concatenate([centre[:, :, :1], centre[:, :, :-1]], axis=2)
    vertical = upper + lower - 2.0 * centre
    east_wind = centre[:, 0:1]
    north_wind = centre[:, 1:2]
    buoyancy = centre[:, 2:3]
    tendency = -(east_wind * slope_x + north_wind * slope_y) + DIFFUSION * laplace + MIXING * vertical
    forcing = jnp.concatenate([CORIOLIS * north_wind, -CORIOLIS * east_wind + BUOYANCY_GAIN * buoyancy,
                               -STRATIFICATION * north_wind, jnp.zeros_like(north_wind)], axis=1)
    updated = centre + TIME_STEP * (tendency + forcing)
    buoyancy_new = updated[:, 2:3]
    moisture = updated[:, 3:4]
    excess = jnp.maximum(moisture - SATURATION * jnp.exp(0.1 * buoyancy_new), 0.0)
    return jnp.concatenate([updated[:, 0:2], buoyancy_new + LATENT * excess, moisture - excess], axis=1)


def advance_all(fields):
    for number in range(STEPS_EACH):
        fields = advance_core(jnp.pad(fields, ((0, 0), (0, 0), (0, 0), (2, 2), (0, 0))))
    return fields


def reference(state, perturbation, ancestors):
    fields = advance_all(state)
    fields = jnp.take(fields, ancestors.astype(jnp.int32), axis=0) + perturbation
    fields = advance_all(fields)
    rows_all = fields.shape[3]
    latitude = jnp.arange(rows_all).astype(jnp.float32)
    weight = 1.0 + 2.0 * latitude / (rows_all - 1)
    buoyancy = fields[:, 2]
    total = jnp.sum(weight[:, None] * buoyancy * buoyancy, axis=(1, 2, 3))
    observable = total / (fields.shape[2] * rows_all * fields.shape[4])
    return fields, observable
```

```python
import functools

import jax
import jax.numpy as jnp
from jax import lax
from jax.experimental import pallas as pl
from jax.experimental.pallas import tpu as pltpu
from jax.sharding import PartitionSpec as P

TIME_STEP = 0.15
DIFFUSION = 0.2
MIXING = 0.1
CORIOLIS = 0.5
BUOYANCY_GAIN = 0.3
STRATIFICATION = 0.3
SATURATION = 0.5
LATENT = 0.5

HALO = 8
PERT_HALO = 8
MESH = pl.DeviceIdType.MESH


def exchange_kernel(tiles, state, pert, other, etop, ebot, ptop, pbot, ssem, rsem):
    t = lax.axis_index("tile")
    m = lax.axis_index("member")
    has_lo = t > 0
    has_hi = t < tiles - 1
    rows = state.shape[3]
    barrier = pltpu.get_barrier_semaphore()
    partner = {"member": 1 - m}
    below = {"tile": t - 1}
    above = {"tile": t + 1}

    pl.semaphore_signal(barrier, inc=1, device_id=partner, device_id_type=MESH)

    @pl.when(has_lo)
    def _():
        pl.semaphore_signal(barrier, inc=1, device_id=below, device_id_type=MESH)

    @pl.when(has_hi)
    def _():
        pl.semaphore_signal(barrier, inc=1, device_id=above, device_id_type=MESH)

    pl.semaphore_wait(barrier, 1 + has_lo.astype(jnp.int32) + has_hi.astype(jnp.int32))

    def remote(src, dst, number, where):
        return pltpu.make_async_remote_copy(
            src_ref=src, dst_ref=dst, send_sem=ssem.at[number], recv_sem=rsem.at[number],
            device_id=where, device_id_type=MESH,
        )

    head = pl.ds(0, HALO)
    tail = pl.ds(rows - HALO, HALO)
    phead = pl.ds(0, PERT_HALO)
    ptail = pl.ds(rows - PERT_HALO, PERT_HALO)
    main = remote(state, other, 0, partner)
    down = remote(state.at[:, :, :, head, :], ebot.at[0], 1, below)
    up = remote(state.at[:, :, :, tail, :], etop.at[0], 2, above)
    pdown = remote(pert.at[:, :, :, phead, :], pbot, 3, below)
    pup = remote(pert.at[:, :, :, ptail, :], ptop, 4, above)
    fbot = remote(ebot.at[0], ebot.at[1], 5, partner)
    ftop = remote(etop.at[0], etop.at[1], 6, partner)

    @pl.when(has_lo)
    def _():
        down.start()

    @pl.when(has_hi)
    def _():
        up.start()

    @pl.when(has_lo)
    def _():
        pdown.start()

    @pl.when(has_hi)
    def _():
        pup.start()

    main.start()

    @pl.when(has_hi)
    def _():
        down.wait_recv()
        fbot.start()

    @pl.when(has_lo)
    def _():
        up.wait_recv()
        ftop.start()

    @pl.when(has_hi)
    def _():
        up.wait_send()
        pup.wait_send()
        pdown.wait_recv()
        fbot.wait()

    @pl.when(has_lo)
    def _():
        down.wait_send()
        pdown.wait_send()
        pup.wait_recv()
        ftop.wait()

    main.wait()


def exchange(state, pert):
    tiles = lax.axis_size("tile")
    lead = state.shape[:3]
    columns = state.shape[4]
    edge = jax.ShapeDtypeStruct((2,) + lead + (HALO, columns), state.dtype)
    pedge = jax.ShapeDtypeStruct(lead + (PERT_HALO, columns), state.dtype)
    anywhere = pl.BlockSpec(memory_space=pl.ANY)
    return pl.pallas_call(
        functools.partial(exchange_kernel, tiles),
        out_shape=[jax.ShapeDtypeStruct(state.shape, state.dtype), edge, edge, pedge, pedge],
        in_specs=[anywhere] * 2,
        out_specs=[anywhere] * 5,
        scratch_shapes=[pltpu.SemaphoreType.DMA((7,)), pltpu.SemaphoreType.DMA((7,))],
        compiler_params=pltpu.CompilerParams(collective_id=0, has_side_effects=True),
        name="exchange",
    )(state, pert)


def advance_block(src, start, columns, emit):
    window = src.at[:, :, pl.ds(pl.multiple_of(start - 8, 8), 24), :]

    def at(field, level, shift):
        return window[field, level, pl.ds(8 + shift, 8), :]

    levels = src.shape[1]
    for level in range(levels):
        centre = [at(field, level, 0) for field in range(4)]
        east, north, buoyancy, _ = centre
        east_scaled = east * (TIME_STEP / 12.0)
        north_scaled = north * (TIME_STEP / 12.0)
        updated = []
        for field in range(4):
            c = centre[field]
            n1 = at(field, level, 1)
            s1 = at(field, level, -1)
            n2 = at(field, level, 2)
            s2 = at(field, level, -2)
            e1 = pltpu.roll(c, columns - 1, 1)
            w1 = pltpu.roll(c, 1, 1)
            e2 = pltpu.roll(c, columns - 2, 1)
            w2 = pltpu.roll(c, 2, 1)
            upper = at(field, level + 1, 0) if level + 1 < levels else c
            lower = at(field, level - 1, 0) if level > 0 else c
            slope_x = 8.0 * (e1 - w1) - (e2 - w2)
            slope_y = 8.0 * (n1 - s1) - (n2 - s2)
            new = c * (1.0 - TIME_STEP * (4.0 * DIFFUSION + 2.0 * MIXING))
            new = new + (TIME_STEP * DIFFUSION) * ((n1 + s1) + (e1 + w1))
            new = new + (TIME_STEP * MIXING) * (upper + lower)
            new = new - (east_scaled * slope_x + north_scaled * slope_y)
            if field == 0:
                new = new + (TIME_STEP * CORIOLIS) * north
            elif field == 1:
                new = new + ((TIME_STEP * BUOYANCY_GAIN) * buoyancy - (TIME_STEP * CORIOLIS) * east)
            elif field == 2:
                new = new - (TIME_STEP * STRATIFICATION) * north
            updated.append(new)
        excess = jnp.maximum(updated[3] - SATURATION * jnp.exp(0.1 * updated[2]), 0.0)
        updated[2] = updated[2] + LATENT * excess
        updated[3] = updated[3] - excess
        for field in range(4):
            emit(field, level, updated[field])


def compute_kernel(total_rows, ancestors, state, other, etop, ebot, pert, ptop, pbot,
                   out, total, a, b, p, o, sems, osem):
    slots, rows, columns = state.shape[0], state.shape[3], state.shape[4]
    t = lax.axis_index("tile")
    owner = lax.axis_index("member")
    has_lo = t > 0
    has_hi = t < lax.axis_size("tile") - 1
    row0 = t * rows
    sources = [ancestors[owner * slots + s] for s in range(slots)]
    holders = [lax.div(source, slots) for source in sources]
    places = [lax.rem(source, slots) for source in sources]
    base = 8 + HALO
    blocks = rows // 8

    def copies(s, where, index):
        source = other if where else state
        return [
            (None, pltpu.make_async_copy(source.at[index], a.at[s, :, :, pl.ds(base, rows), :], sems.at[s, 0])),
            (None, pltpu.make_async_copy(pert.at[s], p.at[s, :, :, pl.ds(base, rows), :], sems.at[s, 1])),
            (has_lo, pltpu.make_async_copy(etop.at[where, index], a.at[s, :, :, pl.ds(8, 8), :], sems.at[s, 2])),
            (has_lo, pltpu.make_async_copy(ptop.at[s], p.at[s, :, :, pl.ds(8, 8), :], sems.at[s, 3])),
            (has_hi, pltpu.make_async_copy(ebot.at[where, index], a.at[s, :, :, pl.ds(base + rows, 8), :], sems.at[s, 4])),
            (has_hi, pltpu.make_async_copy(pbot.at[s], p.at[s, :, :, pl.ds(base + rows, 8), :], sems.at[s, 5])),
        ]

    def start_all(s, where):
        for condition, copy in copies(s, where, places[s]):
            if condition is None:
                copy.start()
            else:
                pl.when(condition)(copy.start)

    for s in range(slots):
        pl.when(holders[s] == owner)(functools.partial(start_all, s, 0))
        pl.when(holders[s] != owner)(functools.partial(start_all, s, 1))

    def clear(ref):
        zero = jnp.zeros(ref.shape[:2] + (8, columns), jnp.float32)

        @pl.when(jnp.logical_not(has_lo))
        def _():
            ref[:, :, pl.ds(8, 8), :] = zero

        @pl.when(jnp.logical_not(has_hi))
        def _():
            ref[:, :, pl.ds(base + rows, 8), :] = zero

    def run_slot(s, carry):
        for condition, copy in copies(s, 0, 0):
            if condition is None:
                copy.wait()
            else:
                pl.when(condition)(copy.wait)
        first, second, bumps, result = a.at[s], b, p.at[s], o.at[s]
        clear(first)

        def plain(src, dst, add):
            def block(i, none):
                start = pl.multiple_of(i * 8, 8)

                def emit(field, level, value):
                    if add is not None:
                        value = value + add[field, level, pl.ds(start, 8), :]
                    dst[field, level, pl.ds(start, 8), :] = value

                advance_block(src, start, columns, emit)
                return none

            lax.fori_loop(1, blocks + 3, block, 0)
            clear(dst)

        plain(first, second, None)
        plain(second, first, bumps)
        plain(first, second, None)

        def last(i, sums):
            start = pl.multiple_of(i * 8, 8)
            there = pl.multiple_of(i * 8 - base, 8)
            row = lax.broadcasted_iota(jnp.int32, (8, columns), 0) + (row0 + there)
            weight = 1.0 + 2.0 * row.astype(jnp.float32) / (total_rows - 1)
            squares = []

            def emit(field, level, value):
                if field == 2:
                    squares.append(value * value)
                result[field, level, pl.ds(there, 8), :] = value

            advance_block(second, start, columns, emit)
            return sums + weight * functools.reduce(jnp.add, squares)

        total[s] = lax.fori_loop(2, blocks + 2, last, jnp.zeros((8, columns), jnp.float32))
        pltpu.make_async_copy(result, out.at[s], osem.at[s]).start()
        return carry

    lax.fori_loop(0, slots, run_slot, 0)
    for s in range(slots):
        pltpu.make_async_copy(o.at[s], out.at[s], osem.at[s]).wait()


def compute(ancestors, state, other, etop, ebot, pert, ptop, pbot, total_rows):
    slots, fields, levels, rows, columns = state.shape
    anywhere = pl.BlockSpec(memory_space=pl.ANY)
    tall = rows + 2 * HALO + 16
    return pl.pallas_call(
        functools.partial(compute_kernel, total_rows),
        out_shape=[
            jax.ShapeDtypeStruct(state.shape, state.dtype),
            jax.ShapeDtypeStruct((slots, 8, columns), jnp.float32),
        ],
        in_specs=[pl.BlockSpec(memory_space=pltpu.SMEM)] + [anywhere] * 7,
        out_specs=[anywhere, pl.BlockSpec(memory_space=pltpu.VMEM)],
        scratch_shapes=[
            pltpu.VMEM((slots, fields, levels, tall, columns), jnp.float32),
            pltpu.VMEM((fields, levels, tall, columns), jnp.float32),
            pltpu.VMEM((slots, fields, levels, tall, columns), jnp.float32),
            pltpu.VMEM((slots, fields, levels, rows, columns), jnp.float32),
            pltpu.SemaphoreType.DMA((slots, 6)),
            pltpu.SemaphoreType.DMA((slots,)),
        ],
        compiler_params=pltpu.CompilerParams(vmem_limit_bytes=61000 * 1024),
        name="advance",
    )(ancestors, state, other, etop, ebot, pert, ptop, pbot)


def reduce_kernel(tiles, partial, total, mine, landed, ssem, rsem):
    t = lax.axis_index("tile")
    barrier = pltpu.get_barrier_semaphore()
    for step in range(1, tiles):
        peer = {"tile": lax.rem(t + step, tiles)}
        pl.semaphore_signal(barrier, inc=1, device_id=peer, device_id_type=MESH)
    summed = jnp.sum(jnp.sum(partial[...], axis=2, keepdims=True), axis=1, keepdims=True)
    mine[...] = jnp.broadcast_to(summed, mine.shape)
    pl.semaphore_wait(barrier, tiles - 1)
    copies = []
    for step in range(1, tiles):
        copies.append(pltpu.make_async_remote_copy(
            src_ref=mine, dst_ref=landed.at[step - 1],
            send_sem=ssem.at[step - 1], recv_sem=rsem.at[step - 1],
            device_id={"tile": lax.rem(t + step, tiles)}, device_id_type=MESH,
        ))
    for copy in copies:
        copy.start()
    for copy in copies:
        copy.wait()
    sums = mine[...]
    for step in range(1, tiles):
        sums = sums + landed[step - 1]
    total[...] = sums


def reduce_tiles(partial):
    tiles = lax.axis_size("tile")
    shape = (partial.shape[0], 8, 128)
    inside = pl.BlockSpec(memory_space=pltpu.VMEM)
    return pl.pallas_call(
        functools.partial(reduce_kernel, tiles),
        out_shape=jax.ShapeDtypeStruct(shape, jnp.float32),
        in_specs=[inside],
        out_specs=inside,
        scratch_shapes=[
            pltpu.VMEM(shape, jnp.float32),
            pltpu.VMEM((tiles - 1,) + shape, jnp.float32),
            pltpu.SemaphoreType.DMA((tiles - 1,)),
            pltpu.SemaphoreType.DMA((tiles - 1,)),
        ],
        compiler_params=pltpu.CompilerParams(collective_id=1, has_side_effects=True),
        name="reduce_tiles",
    )(partial)


def body(state, pert, ancestors):
    slots, fields, levels, rows, columns = state.shape
    tiles = lax.axis_size("tile")
    total_rows = rows * tiles
    other, etop, ebot, ptop, pbot = exchange(state, pert)
    evolved, partial = compute(ancestors, state, other, etop, ebot, pert, ptop, pbot, total_rows)
    total = reduce_tiles(partial)[:, 0, 0]
    return evolved, total / (levels * total_rows * columns)


def solution(mesh):
    spec = P(("groups", "member"), None, None, "tile", None)
    return jax.shard_map(
        body,
        mesh=mesh,
        in_specs=(spec, spec, P("groups")),
        out_specs=(spec, P(("groups", "member"))),
        check_vma=False,
    )
```
